256 devices in a mesh: rep: 8 (over x, core), own: 32 (over y, z).
Axes of the slice: x: 4, y: 4, z: 8, core: 2. Of those that a mesh axis runs over, the one named last changes fastest.
Arguments:
- replica_weights: float32 [8, 64, 512, 512], P('rep', None, 'own'), may hold values from -6 to 6
- global_weights: float32 [64, 512, 512], P(None, 'own'), may hold values from -6 to 6
- momentum: float32 [96, 512, 512], P('own'), may hold values from -4 to 4
- owners: int32 [64], replicated, may hold values from 0 to 31, as said below
Outputs:
- new_weights: float32 [64, 512, 512], P(None, 'own')
- new_momentum: float32 [96, 512, 512], P('own')
The draws below stay inside these ranges and needn't reach their ends.
Inputs may be any that keep to these rules, and one draw needn't show every extreme that they name: `owners`: no device owns more than 3 tiles, and some device owns exactly 3.
All inputs are finite; a program needn't handle non-finite values.
Results may differ from the reference program's by a relative error of at most 0.00016.
Values sent between devices are 32-bit elements; how exact they have to be, the bound alone decides.
A program may use at most 64 MiB of HBM per device.

```python
import jax
import jax.numpy as jnp

TILE_ROWS = 512
TILE_COLS = 512
TILES = 64
CAP = 3
REPLICAS = 8
SLOTS = 96
N_OWN = 32


def draw_owners(key, part):
    key_scores, key_full, key_tiles = jax.random.split(jax.random.fold_in(key, 7), 3)
    slot_total = N_OWN * CAP
    scores = jax.random.permutation(key_scores, slot_total).astype(jnp.int32)
    full_owner = jax.random.randint(key_full, (), 0, N_OWN)
    position = jnp.arange(slot_total, dtype=jnp.int32)
    scores = jnp.where(position // CAP == full_owner, position - slot_total, scores)
    ordered = jnp.argsort(scores, stable=True).astype(jnp.int32)
    chosen = ordered[:TILES] // CAP
    tile_order = jax.random.permutation(key_tiles, TILES)
    return jnp.zeros((TILES,), jnp.int32).at[tile_order].set(chosen.astype(jnp.int32))


def block_scale(stream_key, shape, cuts, least, largest):
    def one(dim, blocks):
        steps = jax.random.uniform(jax.random.fold_in(jax.random.fold_in(stream_key, 6), dim), (blocks,), jnp.float32, least / len(cuts), largest / len(cuts))
        return jnp.repeat(jnp.exp(steps), shape[dim] // blocks).reshape((-1,) + (1,) * (len(shape) - dim - 1))

    factor_of = one(*cuts[0])
    for cut in cuts[1:]:
        factor_of = factor_of * one(*cut)
    return factor_of


def noise(rng, dims, width, limit, pieces=(), held_as=jnp.bfloat16):
    drawn = jax.random.normal(rng, dims, jnp.float32) * width
    if len(pieces) > 0:
        drawn = block_scale(rng, dims, pieces, -0.22, 0.18) * drawn
    return jnp.clip(drawn, min=-limit, max=limit).astype(held_as)


def setup_inputs(seed: int = 0) -> dict:
    key_list = jax.random.split(jax.random.key(seed), 5)
    return {
        "replica_weights": noise(key_list[0], (REPLICAS, TILES, TILE_ROWS, TILE_COLS), 1.0, 6.0, ((0, 8), (2, 32)), jnp.float32),
        "global_weights": noise(key_list[1], (TILES, TILE_ROWS, TILE_COLS), 1.0, 6.0, ((1, 32),), jnp.float32),
        "momentum": noise(key_list[2], (SLOTS, TILE_ROWS, TILE_COLS), 0.5, 4.0, ((0, 32),), jnp.float32),
        "owners": draw_owners(jax.random.fold_in(key_list[4], 71), 0),
    }


outer_rate = 0.7
momentum_decay = 0.5


def slot_ids(owners):
    count = owners.shape[0]
    position = jnp.arange(count, dtype=jnp.int32)
    earlier = (owners[:, None] == owners[None, :]) & (position[None, :] < position[:, None])
    rank = jnp.sum(earlier.astype(jnp.int32), axis=1)
    return (owners * CAP + rank).astype(jnp.int32)


def reference(replica_weights, global_weights, momentum, owners):
    outer_grad = jnp.sum(global_weights[None] - replica_weights, axis=0) / REPLICAS
    slot_id = slot_ids(owners)
    tile_momentum = momentum_decay * momentum[slot_id] + outer_grad
    update = outer_grad + momentum_decay * tile_momentum
    new_weights = global_weights - outer_rate * update
    new_momentum = jnp.zeros_like(momentum).at[slot_id].set(tile_momentum)
    return new_weights, new_momentum
```

```python
import functools

import jax
import jax.numpy as jnp
from jax import lax
from jax.experimental import pallas as pl
from jax.experimental.pallas import tpu as pltpu
from jax.sharding import PartitionSpec as P

outer_rate = 0.7
momentum_decay = 0.5
SUB, LANE = 8, 128
CORES = 2
MESH = pl.DeviceIdType.MESH


def tables(owners, own_count, cap):
    count = owners.shape[0]
    position = jnp.arange(count, dtype=jnp.int32)
    earlier = (owners[:, None] == owners[None, :]) & (position[None, :] < position[:, None])
    slot_id = owners * cap + jnp.sum(earlier.astype(jnp.int32), axis=1)
    hit = slot_id[None, :] == jnp.arange(own_count * cap, dtype=jnp.int32)[:, None]
    tile_of = jnp.sum(jnp.where(hit, position[None, :] + 1, 0), axis=1)
    return slot_id, tile_of


def kernel(
    sizes, slot_ref, tile_ref, r_ref, g_ref, m_ref, w_out, m_out,
    r_mine, r_pair, g_mine, total, far_right, far_left, part_right, part_left, grad, rows_in, m_mine, packed, grad_in,
    w_piece, m_piece,
    load_sem, pair_send, pair_recv, rows_send, rows_recv, grad_send, grad_recv, ring_send, ring_recv,
    w_send, w_recv, w_pair_send, w_pair_recv, m_send, m_recv, m_pair_send, m_pair_recv,
):
    chips, owns, cap, tiles = sizes
    half = tiles // 2
    rep, own = lax.axis_index("rep"), lax.axis_index("own")
    x, core = rep // CORES, rep % CORES
    right, left, far = lax.rem(x + 1, chips), lax.rem(x + chips - 1, chips), lax.rem(x + 2, chips)
    to_right, to_left, to_pair = right * CORES + core, left * CORES + core, x * CORES + 1 - core

    def rows(c):
        return pl.ds(pl.multiple_of(c * SUB, SUB), SUB)

    def cols(q):
        return pl.ds(pl.multiple_of(q * LANE, LANE), LANE)

    order = (far, right, left, x)

    loads = []
    for i, q in enumerate(order):
        a = pltpu.make_async_copy(r_ref.at[0, :, rows(core), cols(q)], r_mine.at[i], load_sem.at[2 * i])
        b = pltpu.make_async_copy(g_ref.at[:, rows(core), cols(q)], g_mine.at[i], load_sem.at[2 * i + 1])
        a.start()
        b.start()
        loads.append((a, b))
    m_load = pltpu.make_async_copy(m_ref.at[:, :, rows(core), cols(x)], m_mine, load_sem.at[8])
    m_load.start()

    barrier = pltpu.get_barrier_semaphore()
    for other in (to_right, to_left, to_pair):
        pl.semaphore_signal(barrier, inc=1, device_id={"rep": other}, device_id_type=MESH)

    def greet(i, carry):
        pl.semaphore_signal(barrier, inc=1, device_id={"own": lax.rem(own + i, owns)}, device_id_type=MESH)
        return carry

    lax.fori_loop(1, owns, greet, 0)
    pl.semaphore_wait(barrier, owns + 2)

    pair = []
    for i, q in enumerate(order):
        copy = pltpu.make_async_remote_copy(
            src_ref=r_ref.at[0, :, rows(1 - core), cols(q)], dst_ref=r_pair.at[i],
            send_sem=pair_send.at[i], recv_sem=pair_recv.at[i], device_id={"rep": to_pair}, device_id_type=MESH,
        )
        copy.start()
        pair.append(copy)

    own_rows = pltpu.make_async_copy(
        m_ref.at[:, own, rows(core), cols(x)], rows_in.at[pl.ds(own * cap, cap)], rows_recv
    )
    own_rows.start()

    def send_rows(i, carry):
        peer = lax.rem(own + i, owns)
        pltpu.make_async_remote_copy(
            src_ref=m_ref.at[:, peer, rows(core), cols(x)], dst_ref=rows_in.at[pl.ds(own * cap, cap)],
            send_sem=rows_send, recv_sem=rows_recv, device_id={"own": peer}, device_id_type=MESH,
        ).start()
        return carry

    lax.fori_loop(1, owns, send_rows, 0)

    def ring(index, src, dst, device):
        return pltpu.make_async_remote_copy(
            src_ref=src, dst_ref=dst, send_sem=ring_send.at[index], recv_sem=ring_recv.at[index],
            device_id={"rep": device}, device_id_type=MESH,
        )

    low, high = pl.ds(0, half), pl.ds(half, half)
    steps = [
        ring(0, total.at[0, low], far_right, to_right),
        ring(1, total.at[0, high], far_left, to_left),
        ring(2, total.at[1, high], part_right.at[high], to_right),
        ring(3, total.at[2, low], part_left.at[low], to_left),
        ring(4, total.at[1, low], part_right.at[low], to_right),
        ring(5, total.at[2, high], part_left.at[high], to_left),
    ]

    for i in range(4):
        loads[i][0].wait()
        loads[i][1].wait()
        pair[i].wait_recv()
        g = g_mine[i]
        total[i] = (g - r_mine[i]) + (g - r_pair[i])
        if i == 0:
            steps[0].start()
            steps[1].start()
        elif i == 1:
            steps[2].start()
        elif i == 2:
            steps[3].start()
    steps[0].wait_recv()
    total[1, low] += far_right[...]
    steps[4].start()
    steps[1].wait_recv()
    total[2, high] += far_left[...]
    steps[5].start()
    for i in (2, 3, 4, 5):
        steps[i].wait_recv()
    scale = 1.0 / (chips * CORES)
    grad[...] = (total[3] + part_right[...] + part_left[...]) * scale

    def pack(s, carry):
        tile = tile_ref[s]
        block = grad[jnp.maximum(tile - 1, 0)]
        packed[s] = jnp.where(tile > 0, block, 0.0)
        return carry

    lax.fori_loop(0, owns * cap, pack, 0, unroll=8)
    own_grad = pltpu.make_async_copy(packed.at[pl.ds(own * cap, cap)], grad_in.at[own], grad_recv)
    own_grad.start()

    def send_grad(i, carry):
        peer = lax.rem(own + i, owns)
        pltpu.make_async_remote_copy(
            src_ref=packed.at[pl.ds(peer * cap, cap)], dst_ref=grad_in.at[own],
            send_sem=grad_send, recv_sem=grad_recv, device_id={"own": peer}, device_id_type=MESH,
        ).start()
        return carry

    lax.fori_loop(1, owns, send_grad, 0)

    def gather(piece, place, n, send, recv, pair_send, pair_recv):
        hn = n // 2

        def over(index, src, dst, device):
            return pltpu.make_async_remote_copy(
                src_ref=src, dst_ref=dst, send_sem=send.at[index], recv_sem=recv.at[index],
                device_id={"rep": device}, device_id_type=MESH,
            )

        def across(index, src, dst):
            return pltpu.make_async_remote_copy(
                src_ref=src, dst_ref=dst, send_sem=pair_send.at[index], recv_sem=pair_recv.at[index],
                device_id={"rep": to_pair}, device_id_type=MESH,
            )

        def view(q, lo):
            return place(q, core, lo, hn)

        mine = [
            over(0, piece(0, hn), view(x, 0), to_right),
            over(1, piece(hn, hn), view(x, hn), to_left),
            over(2, piece(hn, hn), view(x, hn), to_right),
            over(3, piece(0, hn), view(x, 0), to_left),
            across(0, piece(0, n), place(x, core, 0, n)),
        ]
        relays = [over(4, view(left, 0), view(left, 0), to_right), over(5, view(right, hn), view(right, hn), to_left)]
        passes = [
            across(1, view(left, 0), view(left, 0)),
            across(2, view(right, hn), view(right, hn)),
            across(3, view(left, hn), view(left, hn)),
            across(4, view(right, 0), view(right, 0)),
            across(5, view(far, 0), view(far, 0)),
            across(6, view(far, hn), view(far, hn)),
        ]

        def first():
            for copy in mine:
                copy.start()

        def second():
            for i in range(2):
                mine[i].wait_recv()
                relays[i].start()
                passes[i].start()

        def third():
            for i in range(2):
                mine[2 + i].wait_recv()
                passes[2 + i].start()
            for i in range(2):
                relays[i].wait_recv()
                passes[4 + i].start()

        def last():
            for copy in mine + relays:
                copy.wait_send()
            mine[4].wait_recv()
            for copy in passes:
                copy.wait()

        return first, second, third, last

    pltpu.make_async_copy(rows_in, rows_in, rows_recv).wait()

    def weights(k, carry):
        block = grad[k]
        moment = momentum_decay * rows_in[slot_ref[k]] + block
        w_piece[k] = g_mine[3, k] - outer_rate * (block + momentum_decay * moment)
        return carry

    lax.fori_loop(0, tiles, weights, 0, unroll=8)
    w_first, w_second, w_third, w_last = gather(
        lambda lo, n: w_piece.at[pl.ds(lo, n)], lambda q, c, lo, n: w_out.at[pl.ds(lo, n), rows(c), cols(q)], tiles,
        w_send, w_recv, w_pair_send, w_pair_recv,
    )
    w_first()
    w_copy = pltpu.make_async_copy(w_piece, w_out.at[:, rows(core), cols(x)], load_sem.at[9])
    w_copy.start()
    w_second()

    m_load.wait()
    pltpu.make_async_copy(grad_in, grad_in, grad_recv).wait()
    for c in range(cap):
        kept = jnp.where(tile_ref[own * cap + c] > 0, momentum_decay, 0.0)
        m_piece[c] = kept * m_mine[c] + grad_in[:, c]

    def m_place(q, c, lo, n):
        return m_out.at[:, pl.ds(lo, n), rows(c), cols(q)]

    m_first, m_second, m_third, m_last = gather(
        lambda lo, n: m_piece.at[:, pl.ds(lo, n)], m_place, owns, m_send, m_recv, m_pair_send, m_pair_recv
    )
    m_first()
    m_copy = pltpu.make_async_copy(m_piece, m_out.at[:, :, rows(core), cols(x)], load_sem.at[10])
    m_copy.start()
    w_third()
    m_second()
    m_third()

    w_last()
    m_last()
    w_copy.wait()
    m_copy.wait()
    for copy in pair:
        copy.wait_send()
    for copy in steps:
        copy.wait_send()
    sent = pl.ds(0, (owns - 1) * cap)
    pltpu.make_async_copy(rows_in.at[sent], rows_in.at[sent], rows_send).wait()
    pltpu.make_async_copy(packed.at[sent], packed.at[sent], grad_send).wait()


def shards(mesh, replica_weights, global_weights, momentum, owners):
    chips, owns = mesh.shape["rep"] // CORES, mesh.shape["own"]
    tiles, piece_rows, width = global_weights.shape
    cap = momentum.shape[0]
    half = tiles // 2
    slot_id, tile_of = tables(owners, owns, cap)
    momentum = momentum.reshape(cap, owns, piece_rows, width)
    f32 = jnp.float32
    dma = pltpu.SemaphoreType.DMA
    block = (SUB, LANE)
    anywhere = pl.BlockSpec(memory_space=pl.ANY)
    smem = pl.BlockSpec(memory_space=pltpu.SMEM)
    vmem = pl.BlockSpec(memory_space=pltpu.VMEM)
    new_weights, new_momentum = pl.pallas_call(
        functools.partial(kernel, (chips, owns, cap, tiles)),
        out_shape=(
            pltpu.VMEM(global_weights.shape, f32),
            pltpu.VMEM(momentum.shape, f32),
        ),
        in_specs=[smem, smem, anywhere, anywhere, anywhere],
        out_specs=(vmem, vmem),
        scratch_shapes=[
            pltpu.VMEM((4, tiles) + block, f32),
            pltpu.VMEM((4, tiles) + block, f32),
            pltpu.VMEM((4, tiles) + block, f32),
            pltpu.VMEM((4, tiles) + block, f32),
            pltpu.VMEM((half,) + block, f32),
            pltpu.VMEM((half,) + block, f32),
            pltpu.VMEM((tiles,) + block, f32),
            pltpu.VMEM((tiles,) + block, f32),
            pltpu.VMEM((tiles,) + block, f32),
            pltpu.VMEM((owns * cap,) + block, f32),
            pltpu.VMEM((cap, owns) + block, f32),
            pltpu.VMEM((owns * cap,) + block, f32),
            pltpu.VMEM((owns, cap) + block, f32),
            pltpu.VMEM((tiles,) + block, f32),
            pltpu.VMEM((cap, owns) + block, f32),
            dma((11,)), dma((4,)), dma((4,)), dma(()), dma(()), dma(()), dma(()), dma((6,)), dma((6,)),
            dma((6,)), dma((6,)), dma((7,)), dma((7,)), dma((6,)), dma((6,)), dma((7,)), dma((7,)),
        ],
        compiler_params=pltpu.CompilerParams(
            collective_id=0, has_side_effects=True, vmem_limit_bytes=40 * 1024 * 1024
        ),
    )(slot_id, tile_of, replica_weights, global_weights, momentum)
    return new_weights, new_momentum.reshape(cap, owns * piece_rows, width)


def solution(mesh):
    return jax.shard_map(
        functools.partial(shards, mesh),
        mesh=mesh,
        in_specs=(P("rep", None, "own", None), P(None, "own", None), P("own", None, None), P()),
        out_specs=(P(None, "own", None), P("own", None, None)),
        check_vma=False,
    )
```

```python
import functools

import jax
import jax.numpy as jnp
from jax import lax
from jax.experimental import pallas as pl
from jax.experimental.pallas import tpu as pltpu
from jax.sharding import PartitionSpec as P

outer_rate = 0.7
momentum_decay = 0.5
SUB, LANE = 8, 128
CORES = 2
MESH = pl.DeviceIdType.MESH


def tables(owners, slots):
    cap, own_count = slots
    count = owners.shape[1]
    tile = lax.broadcasted_iota(jnp.int32, (count, count), 0)
    other = lax.broadcasted_iota(jnp.int32, (count, count), 1)
    along = jnp.broadcast_to(owners.astype(jnp.float32), (count, count))
    down = jnp.sum(jnp.where(tile == other, along, 0.0), axis=1, keepdims=True)
    same = jnp.where(along == down, 1.0, 0.0)
    slot_along = cap * along[:1] + jnp.sum(jnp.where(tile < other, same, 0.0), axis=0, keepdims=True)
    slot_down = cap * down + jnp.sum(jnp.where(other < tile, same, 0.0), axis=1, keepdims=True)
    place = lax.broadcasted_iota(jnp.int32, (count, LANE), 1).astype(jnp.float32)
    number = lax.broadcasted_iota(jnp.int32, (count, LANE), 0).astype(jnp.float32) + 1.0
    tile_along = jnp.sum(jnp.where(place == slot_down, number, 0.0), axis=0, keepdims=True)
    return slot_along, tile_along


def kernel(
    sizes, owners_ref, r_ref, g_ref, m_ref, w_out, m_out,
    r_mine, r_pair, g_mine, total, far_right, far_left, part_right, part_left, grad, rows_in, m_mine, packed, grad_in,
    w_piece, m_piece, table, slots,
    load_sem, pair_send, pair_recv, rows_send, rows_recv, grad_send, grad_recv, ring_send, ring_recv,
    w_send, w_recv, w_pair_send, w_pair_recv, m_send, m_recv, m_pair_send, m_pair_recv,
):
    chips, owns, cap, tiles = sizes
    half = tiles // 2
    rep, own = lax.axis_index("rep"), lax.axis_index("own")
    x, core = rep // CORES, rep % CORES
    right, left, far = lax.rem(x + 1, chips), lax.rem(x + chips - 1, chips), lax.rem(x + 2, chips)
    to_right, to_left, to_pair = right * CORES + core, left * CORES + core, x * CORES + 1 - core

    def rows(c):
        return pl.ds(pl.multiple_of(c * SUB, SUB), SUB)

    def cols(q):
        return pl.ds(pl.multiple_of(q * LANE, LANE), LANE)

    order = (far, right, left, x)

    loads = []
    for i, q in enumerate(order):
        a = pltpu.make_async_copy(r_ref.at[0, :, rows(core), cols(q)], r_mine.at[i], load_sem.at[2 * i])
        b = pltpu.make_async_copy(g_ref.at[:, rows(core), cols(q)], g_mine.at[i], load_sem.at[2 * i + 1])
        a.start()
        b.start()
        loads.append((a, b))
    m_load = pltpu.make_async_copy(m_ref.at[:, :, rows(core), cols(x)], m_mine, load_sem.at[8])
    m_load.start()

    barrier = pltpu.get_barrier_semaphore()
    for other in (to_right, to_left, to_pair):
        pl.semaphore_signal(barrier, inc=1, device_id={"rep": other}, device_id_type=MESH)

    def greet(i, carry):
        pl.semaphore_signal(barrier, inc=1, device_id={"own": lax.rem(own + i, owns)}, device_id_type=MESH)
        return carry

    lax.fori_loop(1, owns, greet, 0)
    pl.semaphore_wait(barrier, owns + 2)

    pair = []
    for i, q in enumerate(order):
        copy = pltpu.make_async_remote_copy(
            src_ref=r_ref.at[0, :, rows(1 - core), cols(q)], dst_ref=r_pair.at[i],
            send_sem=pair_send.at[i], recv_sem=pair_recv.at[i], device_id={"rep": to_pair}, device_id_type=MESH,
        )
        copy.start()
        pair.append(copy)

    own_rows = pltpu.make_async_copy(
        m_ref.at[:, own, rows(core), cols(x)], rows_in.at[pl.ds(own * cap, cap)], rows_recv
    )
    own_rows.start()

    def send_rows(i, carry):
        peer = lax.rem(own + i, owns)
        pltpu.make_async_remote_copy(
            src_ref=m_ref.at[:, peer, rows(core), cols(x)], dst_ref=rows_in.at[pl.ds(own * cap, cap)],
            send_sem=rows_send, recv_sem=rows_recv, device_id={"own": peer}, device_id_type=MESH,
        ).start()
        return carry

    lax.fori_loop(1, owns, send_rows, 0)

    def ring(index, src, dst, device):
        return pltpu.make_async_remote_copy(
            src_ref=src, dst_ref=dst, send_sem=ring_send.at[index], recv_sem=ring_recv.at[index],
            device_id={"rep": device}, device_id_type=MESH,
        )

    low, high = pl.ds(0, half), pl.ds(half, half)
    steps = [
        ring(0, total.at[0, low], far_right, to_right),
        ring(1, total.at[0, high], far_left, to_left),
        ring(2, total.at[1, high], part_right.at[high], to_right),
        ring(3, total.at[2, low], part_left.at[low], to_left),
        ring(4, total.at[1, low], part_right.at[low], to_right),
        ring(5, total.at[2, high], part_left.at[high], to_left),
    ]

    slot_along, tile_along = tables(owners_ref[...], (cap, owns))
    table[0:1, 0:tiles] = slot_along.astype(jnp.int32)
    table[1:2, :] = tile_along.astype(jnp.int32)
    table_copy = pltpu.make_async_copy(table, slots, load_sem.at[11])
    table_copy.start()

    for i in range(4):
        loads[i][0].wait()
        loads[i][1].wait()
        pair[i].wait_recv()
        g = g_mine[i]
        total[i] = (g - r_mine[i]) + (g - r_pair[i])
        if i == 0:
            steps[0].start()
            steps[1].start()
        elif i == 1:
            steps[2].start()
        elif i == 2:
            steps[3].start()
    steps[0].wait_recv()
    total[1, low] += far_right[...]
    steps[4].start()
    steps[1].wait_recv()
    total[2, high] += far_left[...]
    steps[5].start()
    for i in (2, 3, 4, 5):
        steps[i].wait_recv()
    scale = 1.0 / (chips * CORES)
    grad[...] = (total[3] + part_right[...] + part_left[...]) * scale

    table_copy.wait()

    def pack(s, carry):
        tile = slots[1, s]
        block = grad[jnp.clip(tile - 1, 0, tiles - 1)]
        packed[s] = jnp.where(tile > 0, block, 0.0)
        return carry

    lax.fori_loop(0, owns * cap, pack, 0, unroll=8)
    own_grad = pltpu.make_async_copy(packed.at[pl.ds(own * cap, cap)], grad_in.at[own], grad_recv)
    own_grad.start()

    def send_grad(i, carry):
        peer = lax.rem(own + i, owns)
        pltpu.make_async_remote_copy(
            src_ref=packed.at[pl.ds(peer * cap, cap)], dst_ref=grad_in.at[own],
            send_sem=grad_send, recv_sem=grad_recv, device_id={"own": peer}, device_id_type=MESH,
        ).start()
        return carry

    lax.fori_loop(1, owns, send_grad, 0)

    def gather(piece, place, n, send, recv, pair_send, pair_recv):
        hn = n // 2

        def over(index, src, dst, device):
            return pltpu.make_async_remote_copy(
                src_ref=src, dst_ref=dst, send_sem=send.at[index], recv_sem=recv.at[index],
                device_id={"rep": device}, device_id_type=MESH,
            )

        def across(index, src, dst):
            return pltpu.make_async_remote_copy(
                src_ref=src, dst_ref=dst, send_sem=pair_send.at[index], recv_sem=pair_recv.at[index],
                device_id={"rep": to_pair}, device_id_type=MESH,
            )

        def view(q, lo):
            return place(q, core, lo, hn)

        mine = [
            over(0, piece(0, hn), view(x, 0), to_right),
            over(1, piece(hn, hn), view(x, hn), to_left),
            over(2, piece(hn, hn), view(x, hn), to_right),
            over(3, piece(0, hn), view(x, 0), to_left),
            across(0, piece(0, n), place(x, core, 0, n)),
        ]
        relays = [over(4, view(left, 0), view(left, 0), to_right), over(5, view(right, hn), view(right, hn), to_left)]
        passes = [
            across(1, view(left, 0), view(left, 0)),
            across(2, view(right, hn), view(right, hn)),
            across(3, view(left, hn), view(left, hn)),
            across(4, view(right, 0), view(right, 0)),
            across(5, view(far, 0), view(far, 0)),
            across(6, view(far, hn), view(far, hn)),
        ]

        def first():
            for copy in mine:
                copy.start()

        def second():
            for i in range(2):
                mine[i].wait_recv()
                relays[i].start()
                passes[i].start()

        def third():
            for i in range(2):
                mine[2 + i].wait_recv()
                passes[2 + i].start()
            for i in range(2):
                relays[i].wait_recv()
                passes[4 + i].start()

        def last():
            for copy in mine + relays:
                copy.wait_send()
            mine[4].wait_recv()
            for copy in passes:
                copy.wait()

        return first, second, third, last

    pltpu.make_async_copy(rows_in, rows_in, rows_recv).wait()

    def weights(k, carry):
        block = grad[k]
        moment = momentum_decay * rows_in[jnp.clip(slots[0, k], 0, owns * cap - 1)] + block
        w_piece[k] = g_mine[3, k] - outer_rate * (block + momentum_decay * moment)
        return carry

    lax.fori_loop(0, tiles, weights, 0, unroll=8)
    w_first, w_second, w_third, w_last = gather(
        lambda lo, n: w_piece.at[pl.ds(lo, n)], lambda q, c, lo, n: w_out.at[pl.ds(lo, n), rows(c), cols(q)], tiles,
        w_send, w_recv, w_pair_send, w_pair_recv,
    )
    w_first()
    w_copy = pltpu.make_async_copy(w_piece, w_out.at[:, rows(core), cols(x)], load_sem.at[9])
    w_copy.start()
    w_second()

    m_load.wait()
    pltpu.make_async_copy(grad_in, grad_in, grad_recv).wait()
    for c in range(cap):
        kept = jnp.where(slots[1, own * cap + c] > 0, momentum_decay, 0.0)
        m_piece[c] = kept * m_mine[c] + grad_in[:, c]

    def m_place(q, c, lo, n):
        return m_out.at[:, pl.ds(lo, n), rows(c), cols(q)]

    m_first, m_second, m_third, m_last = gather(
        lambda lo, n: m_piece.at[:, pl.ds(lo, n)], m_place, owns, m_send, m_recv, m_pair_send, m_pair_recv
    )
    m_first()
    m_copy = pltpu.make_async_copy(m_piece, m_out.at[:, :, rows(core), cols(x)], load_sem.at[10])
    m_copy.start()
    w_third()
    m_second()
    m_third()

    w_last()
    m_last()
    w_copy.wait()
    m_copy.wait()
    for copy in pair:
        copy.wait_send()
    for copy in steps:
        copy.wait_send()
    sent = pl.ds(0, (owns - 1) * cap)
    pltpu.make_async_copy(rows_in.at[sent], rows_in.at[sent], rows_send).wait()
    pltpu.make_async_copy(packed.at[sent], packed.at[sent], grad_send).wait()


def shards(mesh, replica_weights, global_weights, momentum, owners):
    chips, owns = mesh.shape["rep"] // CORES, mesh.shape["own"]
    tiles, piece_rows, width = global_weights.shape
    cap = momentum.shape[0]
    half = tiles // 2
    momentum = momentum.reshape(cap, owns, piece_rows, width)
    f32 = jnp.float32
    dma = pltpu.SemaphoreType.DMA
    block = (SUB, LANE)
    space = pltpu.MemorySpace.HBM
    hbm = pl.BlockSpec(memory_space=space)
    vmem = pl.BlockSpec(memory_space=pltpu.VMEM)
    new_weights, new_momentum = pl.pallas_call(
        functools.partial(kernel, (chips, owns, cap, tiles)),
        out_shape=(
            pltpu.VMEM(global_weights.shape, f32),
            pltpu.VMEM(momentum.shape, f32),
        ),
        in_specs=[vmem, hbm, hbm, hbm],
        out_specs=(vmem, vmem),
        scratch_shapes=[
            pltpu.VMEM((4, tiles) + block, f32),
            pltpu.VMEM((4, tiles) + block, f32),
            pltpu.VMEM((4, tiles) + block, f32),
            pltpu.VMEM((4, tiles) + block, f32),
            pltpu.VMEM((half,) + block, f32),
            pltpu.VMEM((half,) + block, f32),
            pltpu.VMEM((tiles,) + block, f32),
            pltpu.VMEM((tiles,) + block, f32),
            pltpu.VMEM((tiles,) + block, f32),
            pltpu.VMEM((owns * cap,) + block, f32),
            pltpu.VMEM((cap, owns) + block, f32),
            pltpu.VMEM((owns * cap,) + block, f32),
            pltpu.VMEM((owns, cap) + block, f32),
            pltpu.VMEM((tiles,) + block, f32),
            pltpu.VMEM((cap, owns) + block, f32),
            pltpu.VMEM((SUB, LANE), jnp.int32),
            pltpu.SMEM((SUB, LANE), jnp.int32),
            dma((12,)), dma((4,)), dma((4,)), dma(()), dma(()), dma(()), dma(()), dma((6,)), dma((6,)),
            dma((6,)), dma((6,)), dma((7,)), dma((7,)), dma((6,)), dma((6,)), dma((7,)), dma((7,)),
        ],
        compiler_params=pltpu.CompilerParams(
            collective_id=0, has_side_effects=True, vmem_limit_bytes=57 * 1024 * 1024
        ),
    )(
        owners.reshape(1, tiles),
        *(pltpu.with_memory_space_constraint(a, space) for a in (replica_weights, global_weights, momentum)),
    )
    return new_weights, new_momentum.reshape(cap, owns * piece_rows, width)


def solution(mesh):
    return jax.shard_map(
        functools.partial(shards, mesh),
        mesh=mesh,
        in_specs=(P("rep", None, "own", None), P(None, "own", None), P("own", None, None), P()),
        out_specs=(P(None, "own", None), P("own", None, None)),
        check_vma=False,
    )
```

```python
import functools

import jax
import jax.numpy as jnp
from jax import lax
from jax.experimental import pallas as pl
from jax.experimental.pallas import tpu as pltpu
from jax.sharding import PartitionSpec as P

outer_rate = 0.7
momentum_decay = 0.5
SUB, LANE = 8, 128
CORES = 2
LINES = 4
DISTANCES = (0, 1, 3, 2)
MESH = pl.DeviceIdType.MESH


def tables(owners, slots):
    cap, own_count = slots
    count = owners.shape[1]
    tile = lax.broadcasted_iota(jnp.int32, (count, count), 0)
    other = lax.broadcasted_iota(jnp.int32, (count, count), 1)
    along = jnp.broadcast_to(owners.astype(jnp.float32), (count, count))
    down = jnp.sum(jnp.where(tile == other, along, 0.0), axis=1, keepdims=True)
    same = jnp.where(along == down, 1.0, 0.0)
    slot_along = cap * along[:1] + jnp.sum(jnp.where(tile < other, same, 0.0), axis=0, keepdims=True)
    slot_down = cap * down + jnp.sum(jnp.where(other < tile, same, 0.0), axis=1, keepdims=True)
    place = lax.broadcasted_iota(jnp.int32, (count, LANE), 1).astype(jnp.float32)
    number = lax.broadcasted_iota(jnp.int32, (count, LANE), 0).astype(jnp.float32) + 1.0
    tile_along = jnp.sum(jnp.where(place == slot_down, number, 0.0), axis=0, keepdims=True)
    return slot_along, tile_along


def kernel(
    sizes, owners_ref, r_ref, g_ref, m_ref, w_out, m_out,
    r_mine, r_pair, g_mine, total, far_right, far_left, part_right, part_left, grad, rows_in, m_mine, packed, grad_in,
    w_piece, m_piece, table, slots,
    load_sem, pair_send, pair_recv, rows_send, rows_recv, grad_send, grad_recv, ring_send, ring_recv,
    w_send, w_recv, w_pair_send, w_pair_recv, m_send, m_recv, m_pair_send, m_pair_recv,
):
    chips, owns, cap, tiles = sizes
    half = tiles // 2
    rep, own = lax.axis_index("rep"), lax.axis_index("own")
    x, core = rep // CORES, rep % CORES
    right, left, far = lax.rem(x + 1, chips), lax.rem(x + chips - 1, chips), lax.rem(x + 2, chips)
    to_right, to_left, to_pair = right * CORES + core, left * CORES + core, x * CORES + 1 - core

    def rows(c):
        return pl.ds(pl.multiple_of(c * SUB, SUB), SUB)

    def cols(q):
        return pl.ds(pl.multiple_of(q * LANE, LANE), LANE)

    order = (far, right, left, x)

    loads = []
    for i, q in enumerate(order):
        a = pltpu.make_async_copy(r_ref.at[0, :, rows(core), cols(q)], r_mine.at[i], load_sem.at[2 * i])
        b = pltpu.make_async_copy(g_ref.at[:, rows(core), cols(q)], g_mine.at[i], load_sem.at[2 * i + 1])
        a.start()
        b.start()
        loads.append((a, b))
    m_load = pltpu.make_async_copy(m_ref.at[:, :, rows(core), cols(x)], m_mine, load_sem.at[8])
    m_load.start()

    barrier = pltpu.get_barrier_semaphore()
    for other in (to_right, to_left, to_pair):
        pl.semaphore_signal(barrier, inc=1, device_id={"rep": other}, device_id_type=MESH)

    def greet(i, carry):
        pl.semaphore_signal(barrier, inc=1, device_id={"own": lax.rem(own + i, owns)}, device_id_type=MESH)
        return carry

    lax.fori_loop(1, owns, greet, 0)
    pl.semaphore_wait(barrier, owns + 2)

    pair = []
    for i, q in enumerate(order):
        copy = pltpu.make_async_remote_copy(
            src_ref=r_ref.at[0, :, rows(1 - core), cols(q)], dst_ref=r_pair.at[i],
            send_sem=pair_send.at[i], recv_sem=pair_recv.at[i], device_id={"rep": to_pair}, device_id_type=MESH,
        )
        copy.start()
        pair.append(copy)

    own_rows = pltpu.make_async_copy(
        m_ref.at[:, own, rows(core), cols(x)], rows_in.at[pl.ds(own * cap, cap)], rows_recv
    )
    own_rows.start()

    def send_rows(i, carry):
        peer = lax.rem(own + i, owns)
        pltpu.make_async_remote_copy(
            src_ref=m_ref.at[:, peer, rows(core), cols(x)], dst_ref=rows_in.at[pl.ds(own * cap, cap)],
            send_sem=rows_send, recv_sem=rows_recv, device_id={"own": peer}, device_id_type=MESH,
        ).start()
        return carry

    lax.fori_loop(1, owns, send_rows, 0)

    def ring(index, src, dst, device):
        return pltpu.make_async_remote_copy(
            src_ref=src, dst_ref=dst, send_sem=ring_send.at[index], recv_sem=ring_recv.at[index],
            device_id={"rep": device}, device_id_type=MESH,
        )

    low, high = pl.ds(0, half), pl.ds(half, half)
    steps = [
        ring(0, total.at[0, low], far_right, to_right),
        ring(1, total.at[0, high], far_left, to_left),
        ring(2, total.at[1, high], part_right.at[high], to_right),
        ring(3, total.at[2, low], part_left.at[low], to_left),
        ring(4, total.at[1, low], part_right.at[low], to_right),
        ring(5, total.at[2, high], part_left.at[high], to_left),
    ]

    slot_along, tile_along = tables(owners_ref[...], (cap, owns))
    table[0:1, 0:tiles] = slot_along.astype(jnp.int32)
    table[1:2, :] = tile_along.astype(jnp.int32)
    table_copy = pltpu.make_async_copy(table, slots, load_sem.at[11])
    table_copy.start()

    for i in range(4):
        loads[i][0].wait()
        loads[i][1].wait()
        pair[i].wait_recv()
        g = g_mine[i]
        total[i] = (g - r_mine[i]) + (g - r_pair[i])
        if i == 0:
            steps[0].start()
            steps[1].start()
        elif i == 1:
            steps[2].start()
        elif i == 2:
            steps[3].start()
    steps[0].wait_recv()
    total[1, low] += far_right[...]
    steps[4].start()
    steps[1].wait_recv()
    total[2, high] += far_left[...]
    steps[5].start()
    for i in (2, 3, 4, 5):
        steps[i].wait_recv()
    scale = 1.0 / (chips * CORES)
    grad[...] = (total[3] + part_right[...] + part_left[...]) * scale

    table_copy.wait()

    def pack(s, carry):
        tile = slots[1, s]
        block = grad[jnp.clip(tile - 1, 0, tiles - 1)]
        packed[s] = jnp.where(tile > 0, block, 0.0)
        return carry

    lax.fori_loop(0, owns * cap, pack, 0, unroll=8)
    own_grad = pltpu.make_async_copy(packed.at[pl.ds(own * cap, cap)], grad_in.at[own], grad_recv.at[0])
    own_grad.start()

    line = owns // LINES
    y, z = own // line, lax.rem(own, line)
    for j in DISTANCES:
        def send_grad(i, carry):
            peer = lax.rem(y + j, LINES) * line + lax.rem(z + i, line)
            pltpu.make_async_remote_copy(
                src_ref=packed.at[pl.ds(peer * cap, cap)], dst_ref=grad_in.at[own],
                send_sem=grad_send, recv_sem=grad_recv.at[j], device_id={"own": peer}, device_id_type=MESH,
            ).start()
            return carry

        lax.fori_loop(1 if j == 0 else 0, line, send_grad, 0)

    def gather(piece, place, n, send, recv, pair_send, pair_recv, group=0):
        hn = n // 2

        def over(index, src, dst, device):
            return pltpu.make_async_remote_copy(
                src_ref=src, dst_ref=dst, send_sem=send.at[6 * group + index], recv_sem=recv.at[6 * group + index],
                device_id={"rep": device}, device_id_type=MESH,
            )

        def across(index, src, dst):
            return pltpu.make_async_remote_copy(
                src_ref=src, dst_ref=dst, send_sem=pair_send.at[7 * group + index],
                recv_sem=pair_recv.at[7 * group + index], device_id={"rep": to_pair}, device_id_type=MESH,
            )

        def view(q, lo):
            return place(q, core, lo, hn)

        mine = [
            over(0, piece(0, hn), view(x, 0), to_right),
            over(1, piece(hn, hn), view(x, hn), to_left),
            over(2, piece(hn, hn), view(x, hn), to_right),
            over(3, piece(0, hn), view(x, 0), to_left),
            across(0, piece(0, n), place(x, core, 0, n)),
        ]
        relays = [over(4, view(left, 0), view(left, 0), to_right), over(5, view(right, hn), view(right, hn), to_left)]
        passes = [
            across(1, view(left, 0), view(left, 0)),
            across(2, view(right, hn), view(right, hn)),
            across(3, view(left, hn), view(left, hn)),
            across(4, view(right, 0), view(right, 0)),
            across(5, view(far, 0), view(far, 0)),
            across(6, view(far, hn), view(far, hn)),
        ]

        def first():
            for copy in mine:
                copy.start()

        def second():
            for i in range(2):
                mine[i].wait_recv()
                relays[i].start()
                passes[i].start()

        def third():
            for i in range(2):
                mine[2 + i].wait_recv()
                passes[2 + i].start()
            for i in range(2):
                relays[i].wait_recv()
                passes[4 + i].start()

        def last():
            for copy in mine + relays:
                copy.wait_send()
            mine[4].wait_recv()
            for copy in passes:
                copy.wait()

        return first, second, third, last

    pltpu.make_async_copy(rows_in, rows_in, rows_recv).wait()

    def weights(k, carry):
        block = grad[k]
        moment = momentum_decay * rows_in[jnp.clip(slots[0, k], 0, owns * cap - 1)] + block
        w_piece[k] = g_mine[3, k] - outer_rate * (block + momentum_decay * moment)
        return carry

    lax.fori_loop(0, tiles, weights, 0, unroll=8)
    w_first, w_second, w_third, w_last = gather(
        lambda lo, n: w_piece.at[pl.ds(lo, n)], lambda q, c, lo, n: w_out.at[pl.ds(lo, n), rows(c), cols(q)], tiles,
        w_send, w_recv, w_pair_send, w_pair_recv,
    )
    w_first()
    w_copy = pltpu.make_async_copy(w_piece, w_out.at[:, rows(core), cols(x)], load_sem.at[9])
    w_copy.start()
    w_second()

    m_load.wait()

    def momentum_chunk(j):
        base = lax.rem(y + LINES - j, LINES) * line
        chunk = pl.ds(base, line)
        pltpu.make_async_copy(grad_in.at[chunk], grad_in.at[chunk], grad_recv.at[j]).wait()
        for c in range(cap):
            kept = jnp.where(slots[1, own * cap + c] > 0, momentum_decay, 0.0)
            m_piece[c, chunk] = kept * m_mine[c, chunk] + grad_in[chunk, c]
        return gather(
            lambda lo, n: m_piece.at[:, pl.ds(base + lo, n)],
            lambda q, c, lo, n: m_out.at[:, pl.ds(base + lo, n), rows(c), cols(q)],
            line, m_send, m_recv, m_pair_send, m_pair_recv, j,
        )

    chunks = []
    for i, j in enumerate(DISTANCES):
        chunks.append(momentum_chunk(j))
        chunks[i][0]()
        if i == 2:
            w_third()
            chunks[0][1]()
    m_copy = pltpu.make_async_copy(m_piece, m_out.at[:, :, rows(core), cols(x)], load_sem.at[10])
    m_copy.start()
    for i in range(LINES):
        if i > 0:
            chunks[i][1]()
            chunks[i - 1][2]()
    chunks[LINES - 1][2]()

    w_last()
    for chunk in chunks:
        chunk[3]()
    w_copy.wait()
    m_copy.wait()
    for copy in pair:
        copy.wait_send()
    for copy in steps:
        copy.wait_send()
    sent = pl.ds(0, (owns - 1) * cap)
    pltpu.make_async_copy(rows_in.at[sent], rows_in.at[sent], rows_send).wait()
    pltpu.make_async_copy(packed.at[sent], packed.at[sent], grad_send).wait()


def shards(mesh, replica_weights, global_weights, momentum, owners):
    chips, owns = mesh.shape["rep"] // CORES, mesh.shape["own"]
    tiles, piece_rows, width = global_weights.shape
    cap = momentum.shape[0]
    half = tiles // 2
    momentum = momentum.reshape(cap, owns, piece_rows, width)
    f32 = jnp.float32
    dma = pltpu.SemaphoreType.DMA
    block = (SUB, LANE)
    space = pltpu.MemorySpace.HBM
    hbm = pl.BlockSpec(memory_space=space)
    vmem = pl.BlockSpec(memory_space=pltpu.VMEM)
    new_weights, new_momentum = pl.pallas_call(
        functools.partial(kernel, (chips, owns, cap, tiles)),
        out_shape=(
            pltpu.VMEM(global_weights.shape, f32),
            pltpu.VMEM(momentum.shape, f32),
        ),
        in_specs=[vmem, hbm, hbm, hbm],
        out_specs=(vmem, vmem),
        scratch_shapes=[
            pltpu.VMEM((4, tiles) + block, f32),
            pltpu.VMEM((4, tiles) + block, f32),
            pltpu.VMEM((4, tiles) + block, f32),
            pltpu.VMEM((4, tiles) + block, f32),
            pltpu.VMEM((half,) + block, f32),
            pltpu.VMEM((half,) + block, f32),
            pltpu.VMEM((tiles,) + block, f32),
            pltpu.VMEM((tiles,) + block, f32),
            pltpu.VMEM((tiles,) + block, f32),
            pltpu.VMEM((owns * cap,) + block, f32),
            pltpu.VMEM((cap, owns) + block, f32),
            pltpu.VMEM((owns * cap,) + block, f32),
            pltpu.VMEM((owns, cap) + block, f32),
            pltpu.VMEM((tiles,) + block, f32),
            pltpu.VMEM((cap, owns) + block, f32),
            pltpu.VMEM((SUB, LANE), jnp.int32),
            pltpu.SMEM((SUB, LANE), jnp.int32),
            dma((12,)), dma((4,)), dma((4,)), dma(()), dma(()), dma(()), dma((LINES,)), dma((6,)), dma((6,)),
            dma((6,)), dma((6,)), dma((7,)), dma((7,)),
            dma((6 * LINES,)), dma((6 * LINES,)), dma((7 * LINES,)), dma((7 * LINES,)),
        ],
        compiler_params=pltpu.CompilerParams(
            collective_id=0, has_side_effects=True, vmem_limit_bytes=57 * 1024 * 1024
        ),
    )(
        owners.reshape(1, tiles),
        *(pltpu.with_memory_space_constraint(a, space) for a in (replica_weights, global_weights, momentum)),
    )
    return new_weights, new_momentum.reshape(cap, owns * piece_rows, width)


def solution(mesh):
    return jax.shard_map(
        functools.partial(shards, mesh),
        mesh=mesh,
        in_specs=(P("rep", None, "own", None), P(None, "own", None), P("own", None, None), P()),
        out_specs=(P(None, "own", None), P("own", None, None)),
        check_vma=False,
    )
```

```python
import functools

import jax
import jax.numpy as jnp
from jax import lax
from jax.experimental import pallas as pl
from jax.experimental.pallas import tpu as pltpu
from jax.sharding import PartitionSpec as P

outer_rate = 0.7
momentum_decay = 0.5
SUB, LANE = 8, 128
CORES = 2
LINES = 4
FAR_Y = (2, 1, 3, 0)
FAR_Z = (4, 3, 5, 2, 6, 1, 7, 0)
MESH = pl.DeviceIdType.MESH


def tables(owners, slots):
    cap, own_count = slots
    count = owners.shape[1]
    tile = lax.broadcasted_iota(jnp.int32, (count, count), 0)
    other = lax.broadcasted_iota(jnp.int32, (count, count), 1)
    along = jnp.broadcast_to(owners.astype(jnp.float32), (count, count))
    down = jnp.sum(jnp.where(tile == other, along, 0.0), axis=1, keepdims=True)
    same = jnp.where(along == down, 1.0, 0.0)
    slot_along = cap * along[:1] + jnp.sum(jnp.where(tile < other, same, 0.0), axis=0, keepdims=True)
    slot_down = cap * down + jnp.sum(jnp.where(other < tile, same, 0.0), axis=1, keepdims=True)
    place = lax.broadcasted_iota(jnp.int32, (count, LANE), 1).astype(jnp.float32)
    number = lax.broadcasted_iota(jnp.int32, (count, LANE), 0).astype(jnp.float32) + 1.0
    tile_along = jnp.sum(jnp.where(place == slot_down, number, 0.0), axis=0, keepdims=True)
    return slot_along, tile_along


def kernel(
    sizes, owners_ref, r_ref, g_ref, m_ref, w_out, m_out,
    r_mine, r_pair, g_mine, total, far_right, far_left, part_right, part_left, grad, rows_in, m_mine, packed, grad_in,
    w_piece, m_piece, table, slots,
    load_sem, pair_send, pair_recv, rows_send, rows_recv, grad_send, grad_recv, ring_send, ring_recv,
    w_send, w_recv, w_pair_send, w_pair_recv, m_send, m_recv, m_pair_send, m_pair_recv,
):
    chips, owns, cap, tiles = sizes
    half = tiles // 2
    rep, own = lax.axis_index("rep"), lax.axis_index("own")
    x, core = rep // CORES, rep % CORES
    right, left, far = lax.rem(x + 1, chips), lax.rem(x + chips - 1, chips), lax.rem(x + 2, chips)
    to_right, to_left, to_pair = right * CORES + core, left * CORES + core, x * CORES + 1 - core

    def rows(c):
        return pl.ds(pl.multiple_of(c * SUB, SUB), SUB)

    def cols(q):
        return pl.ds(pl.multiple_of(q * LANE, LANE), LANE)

    order = (far, right, left, x)

    loads = []
    for i, q in enumerate(order):
        a = pltpu.make_async_copy(r_ref.at[0, :, rows(core), cols(q)], r_mine.at[i], load_sem.at[2 * i])
        b = pltpu.make_async_copy(g_ref.at[:, rows(core), cols(q)], g_mine.at[i], load_sem.at[2 * i + 1])
        a.start()
        b.start()
        loads.append((a, b))
    m_load = pltpu.make_async_copy(m_ref.at[:, :, rows(core), cols(x)], m_mine, load_sem.at[8])
    m_load.start()

    barrier = pltpu.get_barrier_semaphore()
    for other in (to_right, to_left, to_pair):
        pl.semaphore_signal(barrier, inc=1, device_id={"rep": other}, device_id_type=MESH)

    def greet(i, carry):
        pl.semaphore_signal(barrier, inc=1, device_id={"own": lax.rem(own + i, owns)}, device_id_type=MESH)
        return carry

    lax.fori_loop(1, owns, greet, 0)
    pl.semaphore_wait(barrier, owns + 2)

    pair = []
    for i, q in enumerate(order):
        copy = pltpu.make_async_remote_copy(
            src_ref=r_ref.at[0, :, rows(1 - core), cols(q)], dst_ref=r_pair.at[i],
            send_sem=pair_send.at[i], recv_sem=pair_recv.at[i], device_id={"rep": to_pair}, device_id_type=MESH,
        )
        copy.start()
        pair.append(copy)

    own_rows = pltpu.make_async_copy(
        m_ref.at[:, own, rows(core), cols(x)], rows_in.at[pl.ds(own * cap, cap)], rows_recv
    )
    own_rows.start()

    line = owns // LINES
    y, z = own // line, lax.rem(own, line)
    peers = [
        lax.rem(y + dy, LINES) * line + lax.rem(z + dz, line)
        for dz in FAR_Z for dy in FAR_Y if dy or dz
    ]
    for peer in peers:
        pltpu.make_async_remote_copy(
            src_ref=m_ref.at[:, peer, rows(core), cols(x)], dst_ref=rows_in.at[pl.ds(own * cap, cap)],
            send_sem=rows_send, recv_sem=rows_recv, device_id={"own": peer}, device_id_type=MESH,
        ).start()

    def ring(index, src, dst, device):
        return pltpu.make_async_remote_copy(
            src_ref=src, dst_ref=dst, send_sem=ring_send.at[index], recv_sem=ring_recv.at[index],
            device_id={"rep": device}, device_id_type=MESH,
        )

    low, high = pl.ds(0, half), pl.ds(half, half)
    steps = [
        ring(0, total.at[0, low], far_right, to_right),
        ring(1, total.at[0, high], far_left, to_left),
        ring(2, total.at[1, high], part_right.at[high], to_right),
        ring(3, total.at[2, low], part_left.at[low], to_left),
        ring(4, total.at[1, low], part_right.at[low], to_right),
        ring(5, total.at[2, high], part_left.at[high], to_left),
    ]

    slot_along, tile_along = tables(owners_ref[...], (cap, owns))
    table[0:1, 0:tiles] = slot_along.astype(jnp.int32)
    table[1:2, :] = tile_along.astype(jnp.int32)
    table_copy = pltpu.make_async_copy(table, slots, load_sem.at[11])
    table_copy.start()

    for i in range(4):
        loads[i][0].wait()
        loads[i][1].wait()
        pair[i].wait_recv()
        g = g_mine[i]
        total[i] = (g - r_mine[i]) + (g - r_pair[i])
        if i == 0:
            steps[0].start()
            steps[1].start()
        elif i == 1:
            steps[2].start()
        elif i == 2:
            steps[3].start()
    steps[0].wait_recv()
    total[1, low] += far_right[...]
    steps[4].start()
    steps[1].wait_recv()
    total[2, high] += far_left[...]
    steps[5].start()
    for i in (2, 3, 4, 5):
        steps[i].wait_recv()
    scale = 1.0 / (chips * CORES)
    grad[...] = (total[3] + part_right[...] + part_left[...]) * scale

    table_copy.wait()

    def pack(s, carry):
        tile = slots[1, s]
        block = grad[jnp.clip(tile - 1, 0, tiles - 1)]
        packed[s] = jnp.where(tile > 0, block, 0.0)
        return carry

    lax.fori_loop(0, owns * cap, pack, 0, unroll=8)
    own_grad = pltpu.make_async_copy(packed.at[pl.ds(own * cap, cap)], grad_in.at[own], grad_recv)
    own_grad.start()

    for peer in peers:
        pltpu.make_async_remote_copy(
            src_ref=packed.at[pl.ds(peer * cap, cap)], dst_ref=grad_in.at[own],
            send_sem=grad_send, recv_sem=grad_recv, device_id={"own": peer}, device_id_type=MESH,
        ).start()

    def gather(piece, place, n, send, recv, pair_send, pair_recv):
        hn = n // 2

        def over(index, src, dst, device):
            return pltpu.make_async_remote_copy(
                src_ref=src, dst_ref=dst, send_sem=send.at[index], recv_sem=recv.at[index],
                device_id={"rep": device}, device_id_type=MESH,
            )

        def across(index, src, dst):
            return pltpu.make_async_remote_copy(
                src_ref=src, dst_ref=dst, send_sem=pair_send.at[index], recv_sem=pair_recv.at[index],
                device_id={"rep": to_pair}, device_id_type=MESH,
            )

        def view(q, lo):
            return place(q, core, lo, hn)

        mine = [
            over(0, piece(0, hn), view(x, 0), to_right),
            over(1, piece(hn, hn), view(x, hn), to_left),
            over(2, piece(hn, hn), view(x, hn), to_right),
            over(3, piece(0, hn), view(x, 0), to_left),
            across(0, piece(0, n), place(x, core, 0, n)),
        ]
        relays = [over(4, view(left, 0), view(left, 0), to_right), over(5, view(right, hn), view(right, hn), to_left)]
        passes = [
            across(1, view(left, 0), view(left, 0)),
            across(2, view(right, hn), view(right, hn)),
            across(3, view(left, hn), view(left, hn)),
            across(4, view(right, 0), view(right, 0)),
            across(5, view(far, 0), view(far, 0)),
            across(6, view(far, hn), view(far, hn)),
        ]

        def first():
            for copy in mine:
                copy.start()

        def second():
            for i in range(2):
                mine[i].wait_recv()
                relays[i].start()
                passes[i].start()

        def third():
            for i in range(2):
                mine[2 + i].wait_recv()
                passes[2 + i].start()
            for i in range(2):
                relays[i].wait_recv()
                passes[4 + i].start()

        def last():
            for copy in mine + relays:
                copy.wait_send()
            mine[4].wait_recv()
            for copy in passes:
                copy.wait()

        return first, second, third, last

    pltpu.make_async_copy(rows_in, rows_in, rows_recv).wait()

    def weights(k, carry):
        block = grad[k]
        moment = momentum_decay * rows_in[jnp.clip(slots[0, k], 0, owns * cap - 1)] + block
        w_piece[k] = g_mine[3, k] - outer_rate * (block + momentum_decay * moment)
        return carry

    lax.fori_loop(0, tiles, weights, 0, unroll=8)
    w_first, w_second, w_third, w_last = gather(
        lambda lo, n: w_piece.at[pl.ds(lo, n)], lambda q, c, lo, n: w_out.at[pl.ds(lo, n), rows(c), cols(q)], tiles,
        w_send, w_recv, w_pair_send, w_pair_recv,
    )
    w_first()
    w_copy = pltpu.make_async_copy(w_piece, w_out.at[:, rows(core), cols(x)], load_sem.at[9])
    w_copy.start()
    w_second()

    m_load.wait()
    pltpu.make_async_copy(grad_in, grad_in, grad_recv).wait()
    for c in range(cap):
        kept = jnp.where(slots[1, own * cap + c] > 0, momentum_decay, 0.0)
        m_piece[c] = kept * m_mine[c] + grad_in[:, c]

    def m_place(q, c, lo, n):
        return m_out.at[:, pl.ds(lo, n), rows(c), cols(q)]

    m_first, m_second, m_third, m_last = gather(
        lambda lo, n: m_piece.at[:, pl.ds(lo, n)], m_place, owns, m_send, m_recv, m_pair_send, m_pair_recv
    )
    m_first()
    m_copy = pltpu.make_async_copy(m_piece, m_out.at[:, :, rows(core), cols(x)], load_sem.at[10])
    m_copy.start()
    w_third()
    m_second()
    m_third()

    w_last()
    m_last()
    w_copy.wait()
    m_copy.wait()
    for copy in pair:
        copy.wait_send()
    for copy in steps:
        copy.wait_send()
    sent = pl.ds(0, (owns - 1) * cap)
    pltpu.make_async_copy(rows_in.at[sent], rows_in.at[sent], rows_send).wait()
    pltpu.make_async_copy(packed.at[sent], packed.at[sent], grad_send).wait()


def shards(mesh, replica_weights, global_weights, momentum, owners):
    chips, owns = mesh.shape["rep"] // CORES, mesh.shape["own"]
    tiles, piece_rows, width = global_weights.shape
    cap = momentum.shape[0]
    half = tiles // 2
    momentum = momentum.reshape(cap, owns, piece_rows, width)
    f32 = jnp.float32
    dma = pltpu.SemaphoreType.DMA
    block = (SUB, LANE)
    space = pltpu.MemorySpace.HBM
    hbm = pl.BlockSpec(memory_space=space)
    vmem = pl.BlockSpec(memory_space=pltpu.VMEM)
    new_weights, new_momentum = pl.pallas_call(
        functools.partial(kernel, (chips, owns, cap, tiles)),
        out_shape=(
            pltpu.VMEM(global_weights.shape, f32),
            pltpu.VMEM(momentum.shape, f32),
        ),
        in_specs=[vmem, hbm, hbm, hbm],
        out_specs=(vmem, vmem),
        scratch_shapes=[
            pltpu.VMEM((4, tiles) + block, f32),
            pltpu.VMEM((4, tiles) + block, f32),
            pltpu.VMEM((4, tiles) + block, f32),
            pltpu.VMEM((4, tiles) + block, f32),
            pltpu.VMEM((half,) + block, f32),
            pltpu.VMEM((half,) + block, f32),
            pltpu.VMEM((tiles,) + block, f32),
            pltpu.VMEM((tiles,) + block, f32),
            pltpu.VMEM((tiles,) + block, f32),
            pltpu.VMEM((owns * cap,) + block, f32),
            pltpu.VMEM((cap, owns) + block, f32),
            pltpu.VMEM((owns * cap,) + block, f32),
            pltpu.VMEM((owns, cap) + block, f32),
            pltpu.VMEM((tiles,) + block, f32),
            pltpu.VMEM((cap, owns) + block, f32),
            pltpu.VMEM((SUB, LANE), jnp.int32),
            pltpu.SMEM((SUB, LANE), jnp.int32),
            dma((12,)), dma((4,)), dma((4,)), dma(()), dma(()), dma(()), dma(()), dma((6,)), dma((6,)),
            dma((6,)), dma((6,)), dma((7,)), dma((7,)), dma((6,)), dma((6,)), dma((7,)), dma((7,)),
        ],
        compiler_params=pltpu.CompilerParams(
            collective_id=0, has_side_effects=True, vmem_limit_bytes=57 * 1024 * 1024
        ),
    )(
        owners.reshape(1, tiles),
        *(pltpu.with_memory_space_constraint(a, space) for a in (replica_weights, global_weights, momentum)),
    )
    return new_weights, new_momentum.reshape(cap, owns * piece_rows, width)


def solution(mesh):
    return jax.shard_map(
        functools.partial(shards, mesh),
        mesh=mesh,
        in_specs=(P("rep", None, "own", None), P(None, "own", None), P("own", None, None), P()),
        out_specs=(P(None, "own", None), P("own", None, None)),
        check_vma=False,
    )
```

```python
import functools

import jax
import jax.numpy as jnp
from jax import lax
from jax.experimental import pallas as pl
from jax.experimental.pallas import tpu as pltpu
from jax.sharding import PartitionSpec as P

outer_rate = 0.7
momentum_decay = 0.5
SUB, LANE = 8, 128
CORES = 2
MESH = pl.DeviceIdType.MESH


def tables(owners, slots):
    cap, own_count = slots
    count = owners.shape[1]
    tile = lax.broadcasted_iota(jnp.int32, (count, count), 0)
    other = lax.broadcasted_iota(jnp.int32, (count, count), 1)
    along = jnp.broadcast_to(owners.astype(jnp.float32), (count, count))
    down = jnp.sum(jnp.where(tile == other, along, 0.0), axis=1, keepdims=True)
    same = jnp.where(along == down, 1.0, 0.0)
    slot_along = cap * along[:1] + jnp.sum(jnp.where(tile < other, same, 0.0), axis=0, keepdims=True)
    slot_down = cap * down + jnp.sum(jnp.where(other < tile, same, 0.0), axis=1, keepdims=True)
    place = lax.broadcasted_iota(jnp.int32, (count, LANE), 1).astype(jnp.float32)
    number = lax.broadcasted_iota(jnp.int32, (count, LANE), 0).astype(jnp.float32) + 1.0
    tile_along = jnp.sum(jnp.where(place == slot_down, number, 0.0), axis=0, keepdims=True)
    return slot_along, tile_along


def kernel(
    sizes, owners_ref, r_ref, g_ref, m_ref, w_out, m_out,
    r_mine, r_pair, g_mine, total, far_right, far_left, part_right, part_left, grad, rows_in, m_mine, packed, grad_in,
    w_piece, m_piece, table, slots,
    load_sem, pair_send, pair_recv, rows_send, rows_recv, grad_send, grad_recv, ring_send, ring_recv,
    w_send, w_recv, w_pair_send, w_pair_recv, m_send, m_recv, m_pair_send, m_pair_recv,
):
    chips, owns, cap, tiles = sizes
    half = tiles // 2
    rep, own = lax.axis_index("rep"), lax.axis_index("own")
    x, core = rep // CORES, rep % CORES
    right, left, far = lax.rem(x + 1, chips), lax.rem(x + chips - 1, chips), lax.rem(x + 2, chips)
    to_right, to_left, to_pair = right * CORES + core, left * CORES + core, x * CORES + 1 - core

    def rows(c):
        return pl.ds(pl.multiple_of(c * SUB, SUB), SUB)

    def cols(q):
        return pl.ds(pl.multiple_of(q * LANE, LANE), LANE)

    order = (far, right, left, x)

    loads = []
    for i, q in enumerate(order):
        a = pltpu.make_async_copy(r_ref.at[0, :, rows(core), cols(q)], r_mine.at[i], load_sem.at[2 * i])
        b = pltpu.make_async_copy(g_ref.at[:, rows(core), cols(q)], g_mine.at[i], load_sem.at[2 * i + 1])
        a.start()
        b.start()
        loads.append((a, b))
    m_load = pltpu.make_async_copy(m_ref.at[:, :, rows(core), cols(x)], m_mine, load_sem.at[8])
    m_load.start()

    barrier = pltpu.get_barrier_semaphore()
    for other in (to_right, to_left, to_pair):
        pl.semaphore_signal(barrier, inc=1, device_id={"rep": other}, device_id_type=MESH)

    def greet(i, carry):
        pl.semaphore_signal(barrier, inc=1, device_id={"own": lax.rem(own + i, owns)}, device_id_type=MESH)
        return carry

    lax.fori_loop(1, owns, greet, 0)

    slot_along, tile_along = tables(owners_ref[...], (cap, owns))
    table[0:1, 0:tiles] = slot_along.astype(jnp.int32)
    table[1:2, :] = tile_along.astype(jnp.int32)
    table_copy = pltpu.make_async_copy(table, slots, load_sem.at[11])
    table_copy.start()

    pl.semaphore_wait(barrier, owns + 2)

    pair = []
    for i, q in enumerate(order):
        copy = pltpu.make_async_remote_copy(
            src_ref=r_ref.at[0, :, rows(1 - core), cols(q)], dst_ref=r_pair.at[i],
            send_sem=pair_send.at[i], recv_sem=pair_recv.at[i], device_id={"rep": to_pair}, device_id_type=MESH,
        )
        copy.start()
        pair.append(copy)

    own_rows = pltpu.make_async_copy(
        m_ref.at[:, own, rows(core), cols(x)], rows_in.at[pl.ds(own * cap, cap)], rows_recv
    )
    own_rows.start()

    def send_rows(i, carry):
        peer = lax.rem(own + i, owns)
        pltpu.make_async_remote_copy(
            src_ref=m_ref.at[:, peer, rows(core), cols(x)], dst_ref=rows_in.at[pl.ds(own * cap, cap)],
            send_sem=rows_send, recv_sem=rows_recv, device_id={"own": peer}, device_id_type=MESH,
        ).start()
        return carry

    lax.fori_loop(1, owns, send_rows, 0)

    def ring(index, src, dst, device):
        return pltpu.make_async_remote_copy(
            src_ref=src, dst_ref=dst, send_sem=ring_send.at[index], recv_sem=ring_recv.at[index],
            device_id={"rep": device}, device_id_type=MESH,
        )

    low, high = pl.ds(0, half), pl.ds(half, half)
    steps = [
        ring(0, total.at[0, low], far_right, to_right),
        ring(1, total.at[0, high], far_left, to_left),
        ring(2, total.at[1, high], part_right.at[high], to_right),
        ring(3, total.at[2, low], part_left.at[low], to_left),
        ring(4, total.at[1, low], part_right.at[low], to_right),
        ring(5, total.at[2, high], part_left.at[high], to_left),
    ]

    for i in range(4):
        loads[i][0].wait()
        loads[i][1].wait()
        pair[i].wait_recv()
        g = g_mine[i]
        total[i] = (g - r_mine[i]) + (g - r_pair[i])
        if i == 0:
            steps[0].start()
            steps[1].start()
        elif i == 1:
            steps[2].start()
        elif i == 2:
            steps[3].start()
    steps[0].wait_recv()
    total[1, low] += far_right[...]
    steps[4].start()
    steps[1].wait_recv()
    total[2, high] += far_left[...]
    steps[5].start()
    for i in (2, 3, 4, 5):
        steps[i].wait_recv()
    scale = 1.0 / (chips * CORES)
    grad[...] = (total[3] + part_right[...] + part_left[...]) * scale

    table_copy.wait()

    def pack(s, carry):
        tile = slots[1, s]
        block = grad[jnp.clip(tile - 1, 0, tiles - 1)]
        packed[s] = jnp.where(tile > 0, block, 0.0)
        return carry

    lax.fori_loop(0, owns * cap, pack, 0, unroll=8)
    own_grad = pltpu.make_async_copy(packed.at[pl.ds(own * cap, cap)], grad_in.at[own], grad_recv)
    own_grad.start()

    def send_grad(i, carry):
        peer = lax.rem(own + i, owns)
        pltpu.make_async_remote_copy(
            src_ref=packed.at[pl.ds(peer * cap, cap)], dst_ref=grad_in.at[own],
            send_sem=grad_send, recv_sem=grad_recv, device_id={"own": peer}, device_id_type=MESH,
        ).start()
        return carry

    lax.fori_loop(1, owns, send_grad, 0)

    def gather(piece, place, n, send, recv, pair_send, pair_recv):
        hn = n // 2

        def over(index, src, dst, device):
            return pltpu.make_async_remote_copy(
                src_ref=src, dst_ref=dst, send_sem=send.at[index], recv_sem=recv.at[index],
                device_id={"rep": device}, device_id_type=MESH,
            )

        def across(index, src, dst):
            return pltpu.make_async_remote_copy(
                src_ref=src, dst_ref=dst, send_sem=pair_send.at[index], recv_sem=pair_recv.at[index],
                device_id={"rep": to_pair}, device_id_type=MESH,
            )

        def view(q, lo):
            return place(q, core, lo, hn)

        mine = [
            over(0, piece(0, hn), view(x, 0), to_right),
            over(1, piece(hn, hn), view(x, hn), to_left),
            over(2, piece(hn, hn), view(x, hn), to_right),
            over(3, piece(0, hn), view(x, 0), to_left),
            across(0, piece(0, n), place(x, core, 0, n)),
        ]
        relays = [over(4, view(left, 0), view(left, 0), to_right), over(5, view(right, hn), view(right, hn), to_left)]
        passes = [
            across(1, view(left, 0), view(left, 0)),
            across(2, view(right, hn), view(right, hn)),
            across(3, view(left, hn), view(left, hn)),
            across(4, view(right, 0), view(right, 0)),
            across(5, view(far, 0), view(far, 0)),
            across(6, view(far, hn), view(far, hn)),
        ]

        def first():
            for copy in mine:
                copy.start()

        def second():
            for i in range(2):
                mine[i].wait_recv()
                relays[i].start()
                passes[i].start()

        def third():
            for i in range(2):
                mine[2 + i].wait_recv()
                passes[2 + i].start()
            for i in range(2):
                relays[i].wait_recv()
                passes[4 + i].start()

        def last():
            for copy in mine + relays:
                copy.wait_send()
            mine[4].wait_recv()
            for copy in passes:
                copy.wait()

        return first, second, third, last

    pltpu.make_async_copy(rows_in, rows_in, rows_recv).wait()

    def weights(k, carry):
        block = grad[k]
        moment = momentum_decay * rows_in[jnp.clip(slots[0, k], 0, owns * cap - 1)] + block
        w_piece[k] = g_mine[3, k] - outer_rate * (block + momentum_decay * moment)
        return carry

    lax.fori_loop(0, tiles, weights, 0, unroll=8)
    w_first, w_second, w_third, w_last = gather(
        lambda lo, n: w_piece.at[pl.ds(lo, n)], lambda q, c, lo, n: w_out.at[pl.ds(lo, n), rows(c), cols(q)], tiles,
        w_send, w_recv, w_pair_send, w_pair_recv,
    )
    w_first()
    w_copy = pltpu.make_async_copy(w_piece, w_out.at[:, rows(core), cols(x)], load_sem.at[9])
    w_copy.start()
    w_second()

    m_load.wait()
    pltpu.make_async_copy(grad_in, grad_in, grad_recv).wait()
    for c in range(cap):
        kept = jnp.where(slots[1, own * cap + c] > 0, momentum_decay, 0.0)
        m_piece[c] = kept * m_mine[c] + grad_in[:, c]

    def m_place(q, c, lo, n):
        return m_out.at[:, pl.ds(lo, n), rows(c), cols(q)]

    m_first, m_second, m_third, m_last = gather(
        lambda lo, n: m_piece.at[:, pl.ds(lo, n)], m_place, owns, m_send, m_recv, m_pair_send, m_pair_recv
    )
    m_first()
    m_copy = pltpu.make_async_copy(m_piece, m_out.at[:, :, rows(core), cols(x)], load_sem.at[10])
    m_copy.start()
    w_third()
    m_second()
    m_third()

    w_last()
    m_last()
    w_copy.wait()
    m_copy.wait()
    for copy in pair:
        copy.wait_send()
    for copy in steps:
        copy.wait_send()
    sent = pl.ds(0, (owns - 1) * cap)
    pltpu.make_async_copy(rows_in.at[sent], rows_in.at[sent], rows_send).wait()
    pltpu.make_async_copy(packed.at[sent], packed.at[sent], grad_send).wait()


def shards(mesh, replica_weights, global_weights, momentum, owners):
    chips, owns = mesh.shape["rep"] // CORES, mesh.shape["own"]
    tiles, piece_rows, width = global_weights.shape
    cap = momentum.shape[0]
    half = tiles // 2
    momentum = momentum.reshape(cap, owns, piece_rows, width)
    f32 = jnp.float32
    dma = pltpu.SemaphoreType.DMA
    block = (SUB, LANE)
    space = pltpu.MemorySpace.HBM
    hbm = pl.BlockSpec(memory_space=space)
    vmem = pl.BlockSpec(memory_space=pltpu.VMEM)
    new_weights, new_momentum = pl.pallas_call(
        functools.partial(kernel, (chips, owns, cap, tiles)),
        out_shape=(
            pltpu.VMEM(global_weights.shape, f32),
            pltpu.VMEM(momentum.shape, f32),
        ),
        in_specs=[vmem, hbm, hbm, hbm],
        out_specs=(vmem, vmem),
        scratch_shapes=[
            pltpu.VMEM((4, tiles) + block, f32),
            pltpu.VMEM((4, tiles) + block, f32),
            pltpu.VMEM((4, tiles) + block, f32),
            pltpu.VMEM((4, tiles) + block, f32),
            pltpu.VMEM((half,) + block, f32),
            pltpu.VMEM((half,) + block, f32),
            pltpu.VMEM((tiles,) + block, f32),
            pltpu.VMEM((tiles,) + block, f32),
            pltpu.VMEM((tiles,) + block, f32),
            pltpu.VMEM((owns * cap,) + block, f32),
            pltpu.VMEM((cap, owns) + block, f32),
            pltpu.VMEM((owns * cap,) + block, f32),
            pltpu.VMEM((owns, cap) + block, f32),
            pltpu.VMEM((tiles,) + block, f32),
            pltpu.VMEM((cap, owns) + block, f32),
            pltpu.VMEM((SUB, LANE), jnp.int32),
            pltpu.SMEM((SUB, LANE), jnp.int32),
            dma((12,)), dma((4,)), dma((4,)), dma(()), dma(()), dma(()), dma(()), dma((6,)), dma((6,)),
            dma((6,)), dma((6,)), dma((7,)), dma((7,)), dma((6,)), dma((6,)), dma((7,)), dma((7,)),
        ],
        compiler_params=pltpu.CompilerParams(
            collective_id=0, has_side_effects=True, vmem_limit_bytes=57 * 1024 * 1024
        ),
    )(
        owners.reshape(1, tiles),
        *(pltpu.with_memory_space_constraint(a, space) for a in (replica_weights, global_weights, momentum)),
    )
    return new_weights, new_momentum.reshape(cap, owns * piece_rows, width)


def solution(mesh):
    return jax.shard_map(
        functools.partial(shards, mesh),
        mesh=mesh,
        in_specs=(P("rep", None, "own", None), P(None, "own", None), P("own", None, None), P()),
        out_specs=(P(None, "own", None), P("own", None, None)),
        check_vma=False,
    )
```
